32 devices in a mesh: series: 4 (over y, x), tm: 8 (over z, core).
Axes of the slice: x: 2, y: 2, z: 4, core: 2. Of those that a mesh axis runs over, the one named last changes fastest.
Arguments:
- observed: bfloat16 [5120, 6144], P('series', 'tm'), may hold values from -6 to 6
- mask: int32 [5120, 6144], P('series', 'tm'), may hold values 0 or 1
- series_factors: float32 [5120, 256], P('series'), may hold values from -6 to 6
- time_factors: float32 [256, 6144], P(None, 'tm'), may hold values from -0.375 to 0.375
- ar_weights: float32 [3, 256], replicated, may hold values from -0.7 to 0.7
Outputs:
- series_out: float32 [5120, 256], P('series')
- time_out: float32 [256, 6144], P(None, 'tm')
- imputed: bfloat16 [5120, 6144], P('series', 'tm')
The draws below stay inside these ranges and needn't reach their ends.
Inputs may be any that keep to these rules, and one draw needn't show every extreme that they name: mask holds only 0 and 1.
All inputs are finite; a program needn't handle non-finite values. No bound on the sum of `mask` on one device may be relied on, other than what follows from the above.
Results may differ from the reference program's by a relative error of at most 0.0089.
Values sent between devices are 32-bit elements; how exact they have to be, the bound alone decides.
A program may use at most 128 MiB of HBM per device.

```python
import jax
import jax.numpy as jnp
from jax import lax

K = 256
ITERS = 2
SERIES = 5120
HOURS = 6144


def plant(values, stream_key, smallest, largest):
    spot = [jax.random.randint(jax.random.fold_in(stream_key, axis), (), 0, length) for axis, length in enumerate(values.shape)]
    longest = values.shape.index(max(values.shape))
    neighbour = spot[:longest] + [(spot[longest] + 1) % values.shape[longest]] + spot[longest + 1:]
    return values.at[tuple(spot)].set(smallest).at[tuple(neighbour)].set(largest)


def block_scale(stream_key, dims, cuts, least, top_value):
    def one(axis_at, blocks):
        heights = jax.random.uniform(jax.random.fold_in(jax.random.fold_in(stream_key, 6), axis_at), (blocks,), jnp.float32, least / len(cuts), top_value / len(cuts))
        return jnp.repeat(jnp.exp(heights), dims[axis_at] // blocks).reshape((-1,) + (1,) * (len(dims) - axis_at - 1))

    loudness = one(*cuts[0])
    for cut in cuts[1:]:
        loudness = loudness * one(*cut)
    return loudness


def noise(stream_key, dims, deviation, reach, split=(), dtype=jnp.bfloat16):
    values = jax.random.normal(stream_key, dims, jnp.float32) * deviation
    if len(split) > 0:
        values = block_scale(stream_key, dims, split, -0.22, 0.18) * values
    return jnp.clip(values, min=-reach, max=reach).astype(dtype)


def setup_inputs(seed: int = 0) -> dict:
    streams_of = jax.random.split(jax.random.key(seed), 6)
    return {
        "observed": noise(streams_of[0], (SERIES, HOURS), 1.0, 6.0, ((0, 4), (1, 8))),
        "mask": plant((jax.random.randint(streams_of[1], (SERIES, HOURS), 0, 2) < 1).astype(jnp.int32), jax.random.fold_in(streams_of[1], 1), 0, 1),
        "series_factors": noise(streams_of[2], (SERIES, K), 1.0, 6.0, ((0, 4),), jnp.float32),
        "time_factors": noise(streams_of[3], (K, HOURS), K ** -0.5, 0.375, ((1, 8),), jnp.float32),
        "ar_weights": jnp.clip(jax.random.uniform(streams_of[4], (3, K), jnp.float32, -0.7, 0.7), -0.7, 0.7),
    }


lag_hours = (1, 24, 168)


def lag_terms(factors, weights):
    hour_count = factors.shape[1]
    in_range = jnp.arange(hour_count) >= 168
    lag_resid = factors
    for lag_index, lag_size in enumerate(lag_hours):
        earlier = jnp.pad(factors, ((0, 0), (lag_size, 0)))[:, :hour_count]
        lag_resid = lag_resid - weights[lag_index][:, None] * earlier
    lag_resid = jnp.where(in_range[None, :], lag_resid, jnp.zeros_like(lag_resid))
    backward = jnp.zeros_like(lag_resid)
    for lag_index, lag_size in enumerate(lag_hours):
        later = jnp.pad(lag_resid, ((0, 0), (0, lag_size)))[:, lag_size:]
        backward = backward + weights[lag_index][:, None] * later
    return lag_resid, backward


def reference(observed, mask, series_factors, time_factors, ar_weights):
    sensor_count, hour_count = observed.shape
    factor_rank = time_factors.shape[0]
    step_f = factor_rank / hour_count
    step_x = 1.0 / sensor_count
    ridge_f = 0.1 * hour_count / factor_rank
    ridge_x = 0.1 * sensor_count
    lam_ar = sensor_count / 8.0
    series_now = series_factors
    time_now = time_factors
    for sweep in range(ITERS):
        series_low = series_now.astype(jnp.bfloat16)
        time_low = time_now.astype(jnp.bfloat16)
        product = jnp.dot(series_low, time_low, preferred_element_type=jnp.float32)
        misfit = jnp.where(mask != 0, product - observed.astype(jnp.float32), jnp.zeros_like(product)).astype(jnp.bfloat16)
        grad_series = lax.dot_general(misfit, time_low, (((1,), (1,)), ((), ())), preferred_element_type=jnp.float32)
        grad_data = lax.dot_general(series_low, misfit, (((0,), (0,)), ((), ())), preferred_element_type=jnp.float32)
        lag_resid, backward = lag_terms(time_now, ar_weights)
        series_next = series_now - step_f * (grad_series + ridge_f * series_now)
        time_next = time_now - step_x * (grad_data + ridge_x * time_now + lam_ar * (lag_resid - backward))
        series_now, time_now = series_next, time_next
    imputed = jnp.dot(series_now.astype(jnp.bfloat16), time_now.astype(jnp.bfloat16), preferred_element_type=jnp.float32).astype(jnp.bfloat16)
    return series_now, time_now, imputed
```

```python
import functools

import jax
import jax.numpy as jnp
from jax import lax
from jax.experimental import pallas as pl
from jax.experimental.pallas import tpu as pltpu
from jax.sharding import PartitionSpec as P

ITERS = 2
LAGS = (1, 24, 168)
HALO = 256
HALF = 64
BLOCK = 2 * HALF
LAG_STEPS = 4
G_STEP = 8


def kernel(
    series_size, tm_size,
    obs_hbm, mask_hbm, f_in, x_in, w_in,
    f_out, x_out,
    obs, mask, f_new, x_new, misfit, f_low, x_low, grad, partner_in, left_in, right_in,
    g_loc, g_in, halo_l, halo_r, w_cols,
    load_sem, out_sem, pair_send, pair_recv, line_send, left_recv, right_recv,
    out_send, gather_recv, give_send, give_recv, g_send, g_recv, x_send, x_recv,
    edge_send, edge_recv,
):
    rows, rank = f_in.shape
    hours = x_in.shape[1]
    blocks = rows // BLOCK
    piece = rank // series_size
    hours_all = hours * tm_size
    sensors_all = rows * series_size
    step_f = rank / hours_all
    step_x = 1.0 / sensors_all
    ridge_f = 0.1 * hours_all / rank
    ridge_x = 0.1 * sensors_all
    lam_ar = sensors_all / 8.0

    s = lax.axis_index("series")
    tm = lax.axis_index("tm")
    chips = tm_size // 2
    chip, core = tm // 2, tm % 2
    other = 1 - core
    owner = chips // 2 - 1 + core
    partner = chip * 2 + other
    is_owner = chip == owner
    before = chip < owner
    after = chip > owner
    has_left = chip > 0
    has_right = chip < chips - 1
    at_end = jnp.logical_or(jnp.logical_and(before, chip == 0), jnp.logical_and(after, chip == chips - 1))
    relay = jnp.logical_and(jnp.logical_not(is_owner), jnp.logical_not(at_end))

    def both(a, b):
        return jnp.logical_and(a, b)

    def remote(src, dst, ssem, rsem, series_to, tm_to):
        return pltpu.make_async_remote_copy(
            src_ref=src, dst_ref=dst, send_sem=ssem, recv_sem=rsem,
            device_id=(series_to, tm_to), device_id_type=pl.DeviceIdType.MESH,
        )

    def block_rows(b):
        return pl.ds(pl.multiple_of(b * BLOCK, BLOCK), BLOCK)

    def half_rows(b, which):
        return pl.ds(pl.multiple_of(b * BLOCK + which * HALF, HALF), HALF)

    def slot_rows(b):
        return pl.ds(pl.multiple_of(b * HALF, HALF), HALF)

    def piece_rows(i):
        return pl.ds(pl.multiple_of(i * piece, piece), piece)

    def load_copies(b):
        return (
            pltpu.make_async_copy(obs_hbm.at[block_rows(b), :], obs.at[block_rows(b), :], load_sem.at[0, b]),
            pltpu.make_async_copy(mask_hbm.at[block_rows(b), :], mask.at[block_rows(b), :], load_sem.at[1, b]),
        )

    @pl.loop(0, blocks)
    def _(b):
        for c in load_copies(b):
            c.start()

    barrier = pltpu.get_barrier_semaphore()
    for d in (-2, -1, 1, 2):
        @pl.when(both(tm + d >= 0, tm + d < tm_size))
        def _():
            pl.semaphore_signal(barrier, inc=1, device_id=(s, tm + d), device_id_type=pl.DeviceIdType.MESH)
    for d in range(1, series_size):
        pl.semaphore_signal(
            barrier, inc=1, device_id=(lax.rem(s + d, series_size), tm), device_id_type=pl.DeviceIdType.MESH
        )
    pl.semaphore_wait(barrier, series_size - 1 + jnp.minimum(tm, 2) + jnp.minimum(tm_size - 1 - tm, 2))

    def edge_copies(it, source):
        to_right = remote(
            source.at[piece_rows(s), pl.ds(hours - HALO, HALO)], halo_l.at[it],
            edge_send.at[it, 0], edge_recv.at[it, 0], s, tm + 1,
        )
        to_left = remote(
            source.at[piece_rows(s), pl.ds(0, HALO)], halo_r.at[it],
            edge_send.at[it, 1], edge_recv.at[it, 1], s, tm - 1,
        )
        return to_right, to_left

    def start_edges(it, source):
        to_right, to_left = edge_copies(it, source)
        pl.when(tm < tm_size - 1)(to_right.start)
        pl.when(tm > 0)(to_left.start)

    start_edges(0, x_in)
    for lag in range(3):
        w_cols[lag] = jnp.transpose(jnp.broadcast_to(w_in[lag : lag + 1, :], (128, rank)))

    for it in range(ITERS):
        f_now = f_in if it == 0 else f_new.at[it - 1]
        x_now = x_in if it == 0 else x_new.at[it - 1]

        def pair_copy(b, it=it):
            return remote(
                grad.at[it, half_rows(b, other), :], partner_in.at[it, slot_rows(b), :],
                pair_send.at[it, b], pair_recv.at[it, b], s, partner,
            )

        def to_right_copy(b, it=it):
            return remote(
                grad.at[it, half_rows(b, core), :], left_in.at[it, slot_rows(b), :],
                line_send.at[it, b], left_recv.at[it, b], s, tm + 2,
            )

        def to_left_copy(b, it=it):
            return remote(
                grad.at[it, half_rows(b, core), :], right_in.at[it, slot_rows(b), :],
                line_send.at[it, b], right_recv.at[it, b], s, tm - 2,
            )

        def spread_copies(b, it=it):
            rows_own = half_rows(b, core)
            view = f_new.at[it, rows_own, :]
            left = remote(view, view, out_send.at[it, 0, b], gather_recv.at[it, b], s, tm - 2)
            right = remote(view, view, out_send.at[it, 1, b], gather_recv.at[it, b], s, tm + 2)
            give = remote(view, view, give_send.at[it, b], give_recv.at[it, b], s, partner)
            return left, right, give

        def give_wait(b, it=it):
            view = f_new.at[it, half_rows(b, other), :]
            remote(view, view, give_send.at[it, b], give_recv.at[it, b], s, partner).wait_recv()

        def send_inward(b):
            pl.when(before)(to_right_copy(b).start)
            pl.when(after)(to_left_copy(b).start)

        def merge(b):
            pair_copy(b).wait_recv()
            grad[it, half_rows(b, core), :] += partner_in[it, slot_rows(b), :]
            pl.when(at_end)(lambda: send_inward(b))

        x_low[...] = x_now[...].astype(jnp.bfloat16)

        def compute(b, carry):
            if it == 0:
                for c in load_copies(b):
                    c.wait()
            else:
                give_wait(b, it - 1)
            low = f_now[block_rows(b), :].astype(jnp.bfloat16)
            f_low[block_rows(b), :] = low
            product = jnp.dot(low, x_low[...], preferred_element_type=jnp.float32)
            miss = jnp.where(
                mask[block_rows(b), :] != 0,
                product - obs[block_rows(b), :].astype(jnp.float32),
                jnp.zeros_like(product),
            ).astype(jnp.bfloat16)
            misfit[block_rows(b), :] = miss
            grad[it, block_rows(b), :] = lax.dot_general(
                miss, x_low[...], (((1,), (1,)), ((), ())), preferred_element_type=jnp.float32
            )
            pair_copy(b).start()
            pl.when(b > 0)(lambda: merge(b - 1))
            return carry

        lax.fori_loop(0, blocks, compute, 0)
        merge(blocks - 1)

        g_loc[it] = lax.dot_general(
            f_low[...], misfit[...], (((0,), (0,)), ((), ())), preferred_element_type=jnp.float32
        )

        def g_copy(d, it=it):
            to = lax.rem(s + d, series_size)
            return remote(
                g_loc.at[it, piece_rows(to), :], g_in.at[it, d - 1],
                g_send.at[it, d - 1], g_recv.at[it, d - 1], to, tm,
            )

        def x_copy(d, it=it):
            to = lax.rem(s + d, series_size)
            view = x_new.at[it, piece_rows(s), :]
            return remote(view, view, x_send.at[it, d - 1], x_recv.at[it, d - 1], to, tm)

        def x_wait(d, it=it):
            source = lax.rem(s + series_size - d, series_size)
            view = x_new.at[it, piece_rows(source), :]
            remote(view, view, x_send.at[it, d - 1], x_recv.at[it, d - 1], s, tm).wait_recv()

        for d in range(1, series_size):
            g_copy(d).start()

        def relay_step(b):
            @pl.when(both(relay, before))
            def _():
                to_right_copy(b).wait_recv()
                grad[it, half_rows(b, core), :] += left_in[it, slot_rows(b), :]
                to_right_copy(b).start()

            @pl.when(both(relay, after))
            def _():
                to_left_copy(b).wait_recv()
                grad[it, half_rows(b, core), :] += right_in[it, slot_rows(b), :]
                to_left_copy(b).start()

            @pl.when(is_owner)
            def _():
                @pl.when(has_left)
                def _():
                    to_right_copy(b).wait_recv()
                    grad[it, half_rows(b, core), :] += left_in[it, slot_rows(b), :]

                @pl.when(has_right)
                def _():
                    to_left_copy(b).wait_recv()
                    grad[it, half_rows(b, core), :] += right_in[it, slot_rows(b), :]

                old = f_now[half_rows(b, core), :]
                f_new[it, half_rows(b, core), :] = old - step_f * (grad[it, half_rows(b, core), :] + ridge_f * old)
                left, right, give = spread_copies(b)
                pl.when(has_left)(left.start)
                pl.when(has_right)(right.start)
                give.start()

        def spread_step(b):
            left, right, give = spread_copies(b)

            @pl.when(jnp.logical_not(is_owner))
            def _():
                left.wait_recv()
                pl.when(both(before, has_left))(left.start)
                pl.when(both(after, has_right))(right.start)
                give.start()

        def line_step(j, carry):
            pl.when(j < blocks)(lambda: relay_step(j))
            pl.when(j >= LAG_STEPS)(lambda: spread_step(j - LAG_STEPS))
            return carry

        lax.fori_loop(0, G_STEP, line_step, 0)

        to_right, to_left = edge_copies(it, x_now)

        @pl.when(tm > 0)
        def _():
            to_right.wait_recv()

        @pl.when(tm == 0)
        def _():
            halo_l[it] = jnp.zeros_like(halo_l[it])

        @pl.when(tm < tm_size - 1)
        def _():
            to_left.wait_recv()

        @pl.when(tm == tm_size - 1)
        def _():
            halo_r[it] = jnp.zeros_like(halo_r[it])

        own = x_now[piece_rows(s), :]
        extended = jnp.concatenate([halo_l[it], own, halo_r[it]], axis=1)
        width = hours + 2 * HALO
        weights = [w_cols[lag, piece_rows(s), :][:, 0:1] for lag in range(3)]
        resid = extended
        for lag in range(3):
            resid = resid - weights[lag] * pltpu.roll(extended, LAGS[lag], 1)
        hour = lax.broadcasted_iota(jnp.int32, (piece, width), 1) + (tm * hours - HALO)
        resid = jnp.where(both(hour >= 168, hour < hours_all), resid, jnp.zeros_like(resid))
        back = None
        for lag in range(3):
            term = weights[lag] * pltpu.roll(resid, width - LAGS[lag], 1)
            back = term if back is None else back + term
        ar = (resid - back)[:, HALO : HALO + hours]

        total = g_loc[it, piece_rows(s), :]
        for d in range(1, series_size):
            g_copy(d).wait_recv()
            total = total + g_in[it, d - 1]
        x_new[it, piece_rows(s), :] = own - step_x * (total + ridge_x * own + lam_ar * ar)
        for d in range(1, series_size):
            x_copy(d).start()
        if it < ITERS - 1:
            start_edges(it + 1, x_new.at[it])

        lax.fori_loop(G_STEP, blocks + LAG_STEPS, line_step, 0)
        for d in range(1, series_size):
            x_wait(d)

    last = ITERS - 1

    def f_store(b):
        return pltpu.make_async_copy(f_new.at[last, block_rows(b), :], f_out.at[block_rows(b), :], out_sem.at[b])

    x_store = pltpu.make_async_copy(x_new.at[last], x_out, out_sem.at[blocks])
    x_store.start()

    @pl.loop(0, blocks)
    def _(b):
        give_wait(b, last)
        f_store(b).start()

    for it in range(ITERS):
        to_right, to_left = edge_copies(it, x_in if it == 0 else x_new.at[it - 1])
        pl.when(tm < tm_size - 1)(to_right.wait_send)
        pl.when(tm > 0)(to_left.wait_send)
        for d in range(1, series_size):
            to = lax.rem(s + d, series_size)
            remote(
                g_loc.at[it, piece_rows(to), :], g_in.at[it, d - 1],
                g_send.at[it, d - 1], g_recv.at[it, d - 1], to, tm,
            ).wait_send()
            view = x_new.at[it, piece_rows(s), :]
            remote(view, view, x_send.at[it, d - 1], x_recv.at[it, d - 1], to, tm).wait_send()

        @pl.loop(0, blocks)
        def _(b):
            line = grad.at[it, half_rows(b, core), :]
            view = f_new.at[it, half_rows(b, core), :]
            remote(
                grad.at[it, half_rows(b, other), :], partner_in.at[it, slot_rows(b), :],
                pair_send.at[it, b], pair_recv.at[it, b], s, partner,
            ).wait_send()

            @pl.when(jnp.logical_not(is_owner))
            def _():
                remote(line, left_in.at[it, slot_rows(b), :], line_send.at[it, b], left_recv.at[it, b], s, tm).wait_send()

            @pl.when(both(has_left, chip <= owner))
            def _():
                remote(view, view, out_send.at[it, 0, b], gather_recv.at[it, b], s, tm).wait_send()

            @pl.when(both(has_right, chip >= owner))
            def _():
                remote(view, view, out_send.at[it, 1, b], gather_recv.at[it, b], s, tm).wait_send()

            remote(view, view, give_send.at[it, b], give_recv.at[it, b], s, partner).wait_send()

    x_store.wait()

    @pl.loop(0, blocks)
    def _(b):
        f_store(b).wait()


def solution(mesh):
    series_size, tm_size = mesh.shape["series"], mesh.shape["tm"]

    def local(observed, mask, series_factors, time_factors, ar_weights):
        rows, rank = series_factors.shape
        hours = time_factors.shape[1]
        blocks = rows // BLOCK
        piece = rank // series_size
        peers = max(series_size - 1, 1)
        f32, bf16 = jnp.float32, jnp.bfloat16
        vmem = pl.BlockSpec(memory_space=pltpu.VMEM)
        anywhere = pl.BlockSpec(memory_space=pl.ANY)
        dma = pltpu.SemaphoreType.DMA
        half = (ITERS, rows // 2, rank)
        f_last, x_last = pl.pallas_call(
            functools.partial(kernel, series_size, tm_size),
            out_shape=(
                jax.ShapeDtypeStruct((rows, rank), f32),
                jax.ShapeDtypeStruct((rank, hours), f32),
            ),
            in_specs=[anywhere, anywhere, vmem, vmem, vmem],
            out_specs=(anywhere, anywhere),
            scratch_shapes=[
                pltpu.VMEM((rows, hours), bf16),
                pltpu.VMEM((rows, hours), jnp.int32),
                pltpu.VMEM((ITERS, rows, rank), f32),
                pltpu.VMEM((ITERS, rank, hours), f32),
                pltpu.VMEM((rows, hours), bf16),
                pltpu.VMEM((rows, rank), bf16),
                pltpu.VMEM((rank, hours), bf16),
                pltpu.VMEM((ITERS, rows, rank), f32),
                pltpu.VMEM(half, f32),
                pltpu.VMEM(half, f32),
                pltpu.VMEM(half, f32),
                pltpu.VMEM((ITERS, rank, hours), f32),
                pltpu.VMEM((ITERS, peers, piece, hours), f32),
                pltpu.VMEM((ITERS, piece, HALO), f32),
                pltpu.VMEM((ITERS, piece, HALO), f32),
                pltpu.VMEM((3, rank, 128), f32),
                dma((2, blocks)),
                dma((blocks + 1,)),
                dma((ITERS, blocks)), dma((ITERS, blocks)),
                dma((ITERS, blocks)), dma((ITERS, blocks)), dma((ITERS, blocks)),
                dma((ITERS, 2, blocks)), dma((ITERS, blocks)),
                dma((ITERS, blocks)), dma((ITERS, blocks)),
                dma((ITERS, peers)), dma((ITERS, peers)),
                dma((ITERS, peers)), dma((ITERS, peers)),
                dma((ITERS, 2)), dma((ITERS, 2)),
            ],
            compiler_params=pltpu.CompilerParams(
                collective_id=0, has_side_effects=True, vmem_limit_bytes=60 * 1024 * 1024
            ),
        )(observed, mask, series_factors, time_factors, ar_weights)
        imputed = jnp.dot(
            f_last.astype(bf16), x_last.astype(bf16), preferred_element_type=f32
        ).astype(bf16)
        return f_last, x_last, imputed

    in_specs = (P("series", "tm"), P("series", "tm"), P("series", None), P(None, "tm"), P())
    out_specs = (P("series", None), P(None, "tm"), P("series", "tm"))
    return jax.shard_map(local, mesh=mesh, in_specs=in_specs, out_specs=out_specs, check_vma=False)
```

```python
import functools

import jax
import jax.numpy as jnp
from jax import lax
from jax.experimental import pallas as pl
from jax.experimental.pallas import tpu as pltpu
from jax.sharding import PartitionSpec as P

ITERS = 2
LAGS = (1, 24, 168)
HALO = 256
HALF = 64
BLOCK = 2 * HALF
WIDE = 2
TAIL_STEPS = 2
PARTS = 2
LAG_STEPS = 4
EARLY = 0
G_STEPS = ((5, 7), (5, 7))


def kernel(
    series_size, tm_size,
    obs_hbm, mask_hbm, f_hbm, x_hbm, w_in,
    f_out, x_out,
    obs, mask, f_in, x_in, ar, f_new, x_new, misfit, f_low, x_low, grad, partner_in, left_in, right_in,
    g_loc, g_in, halo_l, halo_r, w_cols,
    load_sem, first_sem, out_sem, pair_send, pair_recv, line_send, left_recv, right_recv,
    out_send, gather_recv, give_send, give_recv, g_send, g_recv, x_send, x_recv,
    edge_send, edge_recv,
):
    rows, rank = f_in.shape
    hours = x_in.shape[1]
    blocks = rows // BLOCK
    piece = rank // series_size
    hours_all = hours * tm_size
    sensors_all = rows * series_size
    step_f = rank / hours_all
    step_x = 1.0 / sensors_all
    ridge_f = 0.1 * hours_all / rank
    ridge_x = 0.1 * sensors_all
    lam_ar = sensors_all / 8.0

    s = lax.axis_index("series")
    tm = lax.axis_index("tm")
    chips = tm_size // 2
    chip, core = tm // 2, tm % 2
    other = 1 - core
    owner = chips // 2 - 1 + core
    partner = chip * 2 + other
    is_owner = chip == owner
    before = chip < owner
    after = chip > owner
    has_left = chip > 0
    has_right = chip < chips - 1
    at_end = jnp.logical_or(jnp.logical_and(before, chip == 0), jnp.logical_and(after, chip == chips - 1))
    relay = jnp.logical_and(jnp.logical_not(is_owner), jnp.logical_not(at_end))

    def both(a, b):
        return jnp.logical_and(a, b)

    def remote(src, dst, ssem, rsem, series_to, tm_to):
        return pltpu.make_async_remote_copy(
            src_ref=src, dst_ref=dst, send_sem=ssem, recv_sem=rsem,
            device_id=(series_to, tm_to), device_id_type=pl.DeviceIdType.MESH,
        )

    def block_rows(b):
        return pl.ds(pl.multiple_of(b * BLOCK, BLOCK), BLOCK)

    def half_rows(b, which):
        return pl.ds(pl.multiple_of(b * BLOCK + which * HALF, HALF), HALF)

    def slot_rows(b):
        return pl.ds(pl.multiple_of(b * HALF, HALF), HALF)

    def piece_rows(i):
        return pl.ds(pl.multiple_of(i * piece, piece), piece)

    def load_copies(b):
        return (
            pltpu.make_async_copy(obs_hbm.at[block_rows(b), :], obs.at[block_rows(b), :], load_sem.at[0, b]),
            pltpu.make_async_copy(mask_hbm.at[block_rows(b), :], mask.at[block_rows(b), :], load_sem.at[1, b]),
        )

    f_load = pltpu.make_async_copy(f_hbm, f_in, first_sem.at[0])
    x_load = pltpu.make_async_copy(x_hbm, x_in, first_sem.at[1])
    x_load.start()
    f_load.start()

    @pl.loop(0, blocks)
    def _(b):
        for c in load_copies(b):
            c.start()

    for lag in range(3):
        w_cols[lag] = jnp.transpose(jnp.broadcast_to(w_in[lag : lag + 1, :], (128, rank)))
    x_load.wait()

    barrier = pltpu.get_barrier_semaphore()
    for d in (-2, -1, 1, 2):
        @pl.when(both(tm + d >= 0, tm + d < tm_size))
        def _():
            pl.semaphore_signal(barrier, inc=1, device_id=(s, tm + d), device_id_type=pl.DeviceIdType.MESH)
    for d in range(1, series_size):
        pl.semaphore_signal(
            barrier, inc=1, device_id=(lax.rem(s + d, series_size), tm), device_id_type=pl.DeviceIdType.MESH
        )
    pl.semaphore_wait(barrier, series_size - 1 + jnp.minimum(tm, 2) + jnp.minimum(tm_size - 1 - tm, 2))

    def edge_copies(it, source):
        to_right = remote(
            source.at[piece_rows(s), pl.ds(hours - HALO, HALO)], halo_l.at[it],
            edge_send.at[it, 0], edge_recv.at[it, 0], s, tm + 1,
        )
        to_left = remote(
            source.at[piece_rows(s), pl.ds(0, HALO)], halo_r.at[it],
            edge_send.at[it, 1], edge_recv.at[it, 1], s, tm - 1,
        )
        return to_right, to_left

    def start_edges(it, source):
        to_right, to_left = edge_copies(it, source)
        pl.when(tm < tm_size - 1)(to_right.start)
        pl.when(tm > 0)(to_left.start)

    start_edges(0, x_in)
    f_load.wait()

    spread_done = blocks + EARLY - LAG_STEPS
    earlier_spread = None
    for it in range(ITERS):
        f_now = f_in if it == 0 else f_new.at[it - 1]
        x_now = x_in if it == 0 else x_new.at[it - 1]

        def pair_copy(b, it=it):
            return remote(
                grad.at[it, half_rows(b, other), :], partner_in.at[it, slot_rows(b), :],
                pair_send.at[it, b], pair_recv.at[it, b], s, partner,
            )

        def to_right_copy(b, it=it):
            return remote(
                grad.at[it, half_rows(b, core), :], left_in.at[it, slot_rows(b), :],
                line_send.at[it, b], left_recv.at[it, b], s, tm + 2,
            )

        def to_left_copy(b, it=it):
            return remote(
                grad.at[it, half_rows(b, core), :], right_in.at[it, slot_rows(b), :],
                line_send.at[it, b], right_recv.at[it, b], s, tm - 2,
            )

        def spread_copies(b, it=it):
            rows_own = half_rows(b, core)
            view = f_new.at[it, rows_own, :]
            left = remote(view, view, out_send.at[it, 0, b], gather_recv.at[it, b], s, tm - 2)
            right = remote(view, view, out_send.at[it, 1, b], gather_recv.at[it, b], s, tm + 2)
            give = remote(view, view, give_send.at[it, b], give_recv.at[it, b], s, partner)
            return left, right, give

        def give_wait(b, it=it):
            view = f_new.at[it, half_rows(b, other), :]
            remote(view, view, give_send.at[it, b], give_recv.at[it, b], s, partner).wait_recv()

        def send_inward(b):
            pl.when(before)(to_right_copy(b).start)
            pl.when(after)(to_left_copy(b).start)

        def merge(b):
            pair_copy(b).wait_recv()
            grad[it, half_rows(b, core), :] += partner_in[it, slot_rows(b), :]
            pl.when(at_end)(lambda: send_inward(b))

        x_low[...] = x_now[...].astype(jnp.bfloat16)

        def wide_rows(w):
            return pl.ds(pl.multiple_of(w * WIDE * BLOCK, WIDE * BLOCK), WIDE * BLOCK)

        def row_pass(w, carry, earlier_spread=earlier_spread):
            for part in range(WIDE):
                here = w * WIDE + part
                if it == 0:
                    for c in load_copies(here):
                        c.wait()
                else:
                    pl.when(here >= spread_done)(lambda: earlier_spread(here))
            if it > 0:
                for part in range(WIDE):
                    give_wait(w * WIDE + part, it - 1)
            span = wide_rows(w)
            low = f_now[span, :].astype(jnp.bfloat16)
            f_low[span, :] = low
            product = jnp.dot(low, x_low[...], preferred_element_type=jnp.float32)
            miss = jnp.where(
                mask[span, :] != 0,
                product - obs[span, :].astype(jnp.float32),
                jnp.zeros_like(product),
            ).astype(jnp.bfloat16)
            misfit[span, :] = miss
            grad[it, span, :] = lax.dot_general(
                miss, x_low[...], (((1,), (1,)), ((), ())), preferred_element_type=jnp.float32
            )
            for part in range(WIDE):
                pair_copy(w * WIDE + part).start()

            @pl.when(w > 0)
            def _():
                for part in range(WIDE):
                    merge((w - 1) * WIDE + part)

            return carry

        def columns(part):
            return pl.ds(part * (hours // PARTS), hours // PARTS)

        def g_copy(d, part, it=it):
            to = lax.rem(s + d, series_size)
            return remote(
                g_loc.at[it, piece_rows(to), columns(part)], g_in.at[it, d - 1, :, columns(part)],
                g_send.at[it, part, d - 1], g_recv.at[it, part, d - 1], to, tm,
            )

        def x_copy(d, part, it=it):
            to = lax.rem(s + d, series_size)
            view = x_new.at[it, piece_rows(s), columns(part)]
            return remote(view, view, x_send.at[it, part, d - 1], x_recv.at[it, part, d - 1], to, tm)

        def x_wait(d, part, it=it):
            source = lax.rem(s + series_size - d, series_size)
            view = x_new.at[it, piece_rows(source), columns(part)]
            remote(view, view, x_send.at[it, part, d - 1], x_recv.at[it, part, d - 1], s, tm).wait_recv()

        wide = blocks // WIDE
        lax.fori_loop(0, wide, row_pass, 0)
        for part in range(WIDE):
            merge((wide - 1) * WIDE + part)
        for part in range(PARTS):
            g_loc[it, :, columns(part)] = lax.dot_general(
                f_low[...], misfit[:, columns(part)], (((0,), (0,)), ((), ())),
                preferred_element_type=jnp.float32,
            )
            for d in range(1, series_size):
                g_copy(d, part).start()
        def relay_step(b):
            @pl.when(both(relay, before))
            def _():
                to_right_copy(b).wait_recv()
                grad[it, half_rows(b, core), :] += left_in[it, slot_rows(b), :]
                to_right_copy(b).start()

            @pl.when(both(relay, after))
            def _():
                to_left_copy(b).wait_recv()
                grad[it, half_rows(b, core), :] += right_in[it, slot_rows(b), :]
                to_left_copy(b).start()

            @pl.when(is_owner)
            def _():
                @pl.when(has_left)
                def _():
                    to_right_copy(b).wait_recv()
                    grad[it, half_rows(b, core), :] += left_in[it, slot_rows(b), :]

                @pl.when(has_right)
                def _():
                    to_left_copy(b).wait_recv()
                    grad[it, half_rows(b, core), :] += right_in[it, slot_rows(b), :]

                old = f_now[half_rows(b, core), :]
                f_new[it, half_rows(b, core), :] = old - step_f * (grad[it, half_rows(b, core), :] + ridge_f * old)
                left, right, give = spread_copies(b)
                pl.when(has_left)(left.start)
                pl.when(has_right)(right.start)
                give.start()

        def spread_step(b, spread_copies=spread_copies):
            left, right, give = spread_copies(b)

            @pl.when(jnp.logical_not(is_owner))
            def _():
                left.wait_recv()
                pl.when(both(before, has_left))(left.start)
                pl.when(both(after, has_right))(right.start)
                give.start()

        def line_step(j, carry):
            pl.when(j < blocks)(lambda: relay_step(j))
            pl.when(j >= LAG_STEPS)(lambda: spread_step(j - LAG_STEPS))
            return carry

        to_right, to_left = edge_copies(it, x_now)

        @pl.when(tm > 0)
        def _():
            to_right.wait_recv()

        @pl.when(tm == 0)
        def _():
            halo_l[it] = jnp.zeros_like(halo_l[it])

        @pl.when(tm < tm_size - 1)
        def _():
            to_left.wait_recv()

        @pl.when(tm == tm_size - 1)
        def _():
            halo_r[it] = jnp.zeros_like(halo_r[it])

        own = x_now[piece_rows(s), :]
        extended = jnp.concatenate([halo_l[it], own, halo_r[it]], axis=1)
        width = hours + 2 * HALO
        weights = [w_cols[lag, piece_rows(s), :][:, 0:1] for lag in range(3)]
        resid = extended
        for lag in range(3):
            resid = resid - weights[lag] * pltpu.roll(extended, LAGS[lag], 1)
        hour = lax.broadcasted_iota(jnp.int32, (piece, width), 1) + (tm * hours - HALO)
        resid = jnp.where(both(hour >= 168, hour < hours_all), resid, jnp.zeros_like(resid))
        back = None
        for lag in range(3):
            term = weights[lag] * pltpu.roll(resid, width - LAGS[lag], 1)
            back = term if back is None else back + term
        ar[...] = (resid - back)[:, HALO : HALO + hours]

        done = 0
        for part in range(PARTS):
            lax.fori_loop(done, G_STEPS[it][part], line_step, 0)
            done = G_STEPS[it][part]
            total = g_loc[it, piece_rows(s), columns(part)]
            for d in range(1, series_size):
                g_copy(d, part).wait_recv()
                total = total + g_in[it, d - 1, :, columns(part)]
            old = x_now[piece_rows(s), columns(part)]
            x_new[it, piece_rows(s), columns(part)] = old - step_x * (
                total + ridge_x * old + lam_ar * ar[:, columns(part)]
            )
            for d in range(1, series_size):
                x_copy(d, part).start()
        if it < ITERS - 1:
            start_edges(it + 1, x_new.at[it])

        lax.fori_loop(done, blocks + (LAG_STEPS if it == ITERS - 1 else EARLY), line_step, 0)
        earlier_spread = spread_step
        for part in range(PARTS):
            for d in range(1, series_size):
                x_wait(d, part)

    last = ITERS - 1

    def f_store(b):
        return pltpu.make_async_copy(f_new.at[last, block_rows(b), :], f_out.at[block_rows(b), :], out_sem.at[b])

    x_store = pltpu.make_async_copy(x_new.at[last], x_out, out_sem.at[blocks])
    x_store.start()

    @pl.loop(0, blocks)
    def _(b):
        give_wait(b, last)
        f_store(b).start()

    for it in range(ITERS):
        to_right, to_left = edge_copies(it, x_in if it == 0 else x_new.at[it - 1])
        pl.when(tm < tm_size - 1)(to_right.wait_send)
        pl.when(tm > 0)(to_left.wait_send)
        for d in range(1, series_size):
            to = lax.rem(s + d, series_size)
            for part in range(PARTS):
                span = pl.ds(part * (hours // PARTS), hours // PARTS)
                remote(
                    g_loc.at[it, piece_rows(to), span], g_in.at[it, d - 1, :, span],
                    g_send.at[it, part, d - 1], g_recv.at[it, part, d - 1], to, tm,
                ).wait_send()
                view = x_new.at[it, piece_rows(s), span]
                remote(view, view, x_send.at[it, part, d - 1], x_recv.at[it, part, d - 1], to, tm).wait_send()

        @pl.loop(0, blocks)
        def _(b):
            line = grad.at[it, half_rows(b, core), :]
            view = f_new.at[it, half_rows(b, core), :]
            remote(
                grad.at[it, half_rows(b, other), :], partner_in.at[it, slot_rows(b), :],
                pair_send.at[it, b], pair_recv.at[it, b], s, partner,
            ).wait_send()

            @pl.when(jnp.logical_not(is_owner))
            def _():
                remote(line, left_in.at[it, slot_rows(b), :], line_send.at[it, b], left_recv.at[it, b], s, tm).wait_send()

            @pl.when(both(has_left, chip <= owner))
            def _():
                remote(view, view, out_send.at[it, 0, b], gather_recv.at[it, b], s, tm).wait_send()

            @pl.when(both(has_right, chip >= owner))
            def _():
                remote(view, view, out_send.at[it, 1, b], gather_recv.at[it, b], s, tm).wait_send()

            remote(view, view, give_send.at[it, b], give_recv.at[it, b], s, partner).wait_send()

    x_store.wait()

    @pl.loop(0, blocks)
    def _(b):
        f_store(b).wait()


def final_product(f_ref, x_ref, f_out, x_out, imputed, x_low):
    @pl.when(pl.program_id(0) == 0)
    def _():
        x_out[...] = x_ref[...]
        x_low[...] = x_ref[...].astype(jnp.bfloat16)

    f_out[...] = f_ref[...]
    imputed[...] = jnp.dot(
        f_ref[...].astype(jnp.bfloat16), x_low[...], preferred_element_type=jnp.float32
    ).astype(jnp.bfloat16)


def solution(mesh):
    series_size, tm_size = mesh.shape["series"], mesh.shape["tm"]

    def local(observed, mask, series_factors, time_factors, ar_weights):
        rows, rank = series_factors.shape
        hours = time_factors.shape[1]
        blocks = rows // BLOCK
        piece = rank // series_size
        peers = max(series_size - 1, 1)
        f32, bf16 = jnp.float32, jnp.bfloat16
        vmem = pl.BlockSpec(memory_space=pltpu.VMEM)
        anywhere = pl.BlockSpec(memory_space=pl.ANY)
        dma = pltpu.SemaphoreType.DMA
        half = (ITERS, rows // 2, rank)
        f_last, x_last = pl.pallas_call(
            functools.partial(kernel, series_size, tm_size),
            out_shape=(
                jax.ShapeDtypeStruct((rows, rank), f32),
                jax.ShapeDtypeStruct((rank, hours), f32),
            ),
            in_specs=[anywhere, anywhere, anywhere, anywhere, vmem],
            out_specs=(anywhere, anywhere),
            scratch_shapes=[
                pltpu.VMEM((rows, hours), bf16),
                pltpu.VMEM((rows, hours), jnp.int32),
                pltpu.VMEM((rows, rank), f32),
                pltpu.VMEM((rank, hours), f32),
                pltpu.VMEM((piece, hours), f32),
                pltpu.VMEM((ITERS, rows, rank), f32),
                pltpu.VMEM((ITERS, rank, hours), f32),
                pltpu.VMEM((rows, hours), bf16),
                pltpu.VMEM((rows, rank), bf16),
                pltpu.VMEM((rank, hours), bf16),
                pltpu.VMEM((ITERS, rows, rank), f32),
                pltpu.VMEM(half, f32),
                pltpu.VMEM(half, f32),
                pltpu.VMEM(half, f32),
                pltpu.VMEM((ITERS, rank, hours), f32),
                pltpu.VMEM((ITERS, peers, piece, hours), f32),
                pltpu.VMEM((ITERS, piece, HALO), f32),
                pltpu.VMEM((ITERS, piece, HALO), f32),
                pltpu.VMEM((3, rank, 128), f32),
                dma((2, blocks)),
                dma((2,)),
                dma((blocks + 1,)),
                dma((ITERS, blocks)), dma((ITERS, blocks)),
                dma((ITERS, blocks)), dma((ITERS, blocks)), dma((ITERS, blocks)),
                dma((ITERS, 2, blocks)), dma((ITERS, blocks)),
                dma((ITERS, blocks)), dma((ITERS, blocks)),
                dma((ITERS, PARTS, peers)), dma((ITERS, PARTS, peers)),
                dma((ITERS, PARTS, peers)), dma((ITERS, PARTS, peers)),
                dma((ITERS, 2)), dma((ITERS, 2)),
            ],
            compiler_params=pltpu.CompilerParams(
                collective_id=0, has_side_effects=True, vmem_limit_bytes=60 * 1024 * 1024
            ),
        )(observed, mask, series_factors, time_factors, ar_weights)
        tall = rows // TAIL_STEPS
        by_row = lambda width: pl.BlockSpec((tall, width), lambda i: (i, 0))
        whole = pl.BlockSpec((rank, hours), lambda i: (0, 0))
        return tuple(pl.pallas_call(
            final_product,
            grid=(TAIL_STEPS,),
            out_shape=(
                jax.ShapeDtypeStruct((rows, rank), f32),
                jax.ShapeDtypeStruct((rank, hours), f32),
                jax.ShapeDtypeStruct((rows, hours), bf16),
            ),
            in_specs=[by_row(rank), whole],
            out_specs=(by_row(rank), whole, by_row(hours)),
            scratch_shapes=[pltpu.VMEM((rank, hours), bf16)],
        )(f_last, x_last))

    in_specs = (P("series", "tm"), P("series", "tm"), P("series", None), P(None, "tm"), P())
    out_specs = (P("series", None), P(None, "tm"), P("series", "tm"))
    return jax.shard_map(local, mesh=mesh, in_specs=in_specs, out_specs=out_specs, check_vma=False)
```
